32 devices in a mesh: groups: 2 (over x), rows: 8 (over z, y), chan: 2 (over core).
Axes of the slice: x: 2, y: 2, z: 4, core: 2. Of those that a mesh axis runs over, the one named last changes fastest.
Arguments:
- latents: bfloat16 [48, 32, 1024], P('groups', 'rows', 'chan'), parts along dimension 0, may hold values from -6 to 6
- timestep: int32 [6], P('groups'), parts along dimension 0, may hold values from 0 to 999
- label: int32 [6], P('groups'), parts along dimension 0, may hold values from 0 to 15
- time_table: bfloat16 [1000, 1024], P(None, 'chan'), may hold values from -3 to 3
- class_table: bfloat16 [16, 1024], replicated, may hold values from -6 to 6
- dw_kernel: bfloat16 [7, 7, 1024], P(None, None, 'chan'), may hold values from -0.875 to 0.875
- dw_bias: bfloat16 [1024], P('chan'), may hold values from -3 to 3
- ln_gain: bfloat16 [1024], P('chan'), may hold values from 0.25 to 1.75
- ln_bias: bfloat16 [1024], P('chan'), may hold values from -2 to 2
- up_weight: bfloat16 [1024, 4096], P(None, 'chan'), may hold values from -0.1875 to 0.1875
- up_bias: bfloat16 [4096], P('chan'), may hold values from -3 to 3
- down_weight: bfloat16 [4096, 1024], P('chan'), may hold values from -0.09375 to 0.09375
- down_bias: bfloat16 [1024], P('chan'), may hold values from -3 to 3
- layer_scale: bfloat16 [1024], replicated, may hold values from 0.5 to 1.5
Outputs:
- features: bfloat16 [48, 32, 1024], P(('groups', 'rows'), None, 'chan'), parts along dimension 0
- gradient: float32 [48, 32, 1024], P('groups', 'rows', 'chan'), parts along dimension 0
The draws below stay inside these ranges and needn't reach their ends.
There are 2 independent parts, one for each index of `groups`. The reference program is written for one: setup_inputs(seed, part) draws one part's arguments, and reference() takes and returns one part's arrays. A program takes and returns all parts, laid end to end along the dimension named above; an argument that names none is the same for every part. Nothing has to cross between parts.
Inputs may be any that keep to these rules, and one draw needn't show every extreme that they name: One timestep index for each image, a row of the table of 1000 timesteps. `label`: one defect class for each image, out of 16 classes.
All inputs are finite; a program needn't handle non-finite values.
Results may differ from the reference program's by a relative error of at most 0.0045.
Values may be sent and summed in bfloat16 or wider, within the bound.
No kernel may reach another device: no remote copies, remote signals or barrier semaphores. Data moves between devices by JAX's collectives and lax.ppermute only.
A program may use at most 128 MiB of HBM per device.

```python
import jax
import jax.numpy as jnp
from jax import lax

C = 1024
HID = 4096
NT = 1000
NCLS = 16
IMGS = 3
H = 24
W = 32
IH = 8


def shard_levels(key, shape, pieces, least, high):
    def one(axis_at, blocks):
        draws = jax.random.uniform(jax.random.fold_in(jax.random.fold_in(key, 6), axis_at), (blocks,), jnp.float32, least / len(pieces), high / len(pieces))
        return jnp.repeat(jnp.exp(draws), shape[axis_at] // blocks).reshape((-1,) + (1,) * (len(shape) - axis_at - 1))

    level = one(*pieces[0])
    for cut in pieces[1:]:
        level = level * one(*cut)
    return level


def centred(key, dims, deviation, bound, split=(), kind=jnp.bfloat16):
    level = shard_levels(key, dims, split, -0.22, 0.18) if split else 1.0
    drawn = jax.random.normal(key, dims, jnp.float32) * deviation * level
    return jnp.minimum(jnp.maximum(drawn, -bound), bound).astype(kind)


def setup_inputs(seed: int = 0, part: int = 0) -> dict:
    streams_of = jax.random.split(jax.random.key(seed), 15)
    part_keys = jax.random.split(jax.random.fold_in(streams_of[14], part), 15)
    return {
        "latents": centred(part_keys[0], (H, W, C), 1.0, 6.0, ((1, 8), (2, 2))),
        "timestep": jax.random.randint(part_keys[1], (IMGS,), 0, NT).astype(jnp.int32),
        "label": jax.random.randint(part_keys[2], (IMGS,), 0, NCLS).astype(jnp.int32),
        "time_table": centred(streams_of[3], (NT, C), 0.5, 3.0, ((1, 2),)),
        "class_table": centred(streams_of[4], (NCLS, C), 1.0, 6.0),
        "dw_kernel": centred(streams_of[5], (7, 7, C), 49 ** -0.5, 0.875, ((2, 2),)),
        "dw_bias": centred(streams_of[6], (C,), 0.5, 3.0, ((0, 2),)),
        "ln_gain": jnp.clip(1.0 + 0.15 * jax.random.normal(streams_of[7], (C,), jnp.float32), 0.25, 1.75).astype(jnp.bfloat16),
        "ln_bias": centred(streams_of[8], (C,), 0.3, 2.0, ((0, 2),)),
        "up_weight": centred(streams_of[9], (C, HID), C ** -0.5, 0.1875, ((1, 2),)),
        "up_bias": centred(streams_of[10], (HID,), 0.5, 3.0, ((0, 2),)),
        "down_weight": centred(streams_of[11], (HID, C), HID ** -0.5, 0.09375, ((0, 2),)),
        "down_bias": centred(streams_of[12], (C,), 0.5, 3.0, ((0, 2),)),
        "layer_scale": jnp.clip(jax.random.uniform(streams_of[13], (C,), jnp.float32, 0.5, 1.5), 0.5, 1.5).astype(jnp.bfloat16),
    }


KAPPA = 0.7978845608028654
EPSILON = 1e-06

def gelu_tanh(values):
    inner = KAPPA * (values + 0.044715 * values * values * values)
    return 0.5 * values * (1.0 + jnp.tanh(inner))

def gelu_slope(values):
    tangent = jnp.tanh(KAPPA * (values + 0.044715 * values * values * values))
    return 0.5 * (1.0 + tangent) + 0.5 * values * (1.0 - tangent * tangent) * KAPPA * (1.0 + 3.0 * 0.044715 * values * values)

def stencil(padded, kernel, masks):
    height = padded.shape[0] - 6
    width = padded.shape[1] - 6
    total = jnp.zeros((height, width, padded.shape[2]), jnp.float32)
    for row_tap in range(7):
        partial_row = jnp.zeros((height, width, padded.shape[2]), jnp.float32)
        for col_tap in range(7):
            partial_row = partial_row + padded[row_tap:row_tap + height, col_tap:col_tap + width, :] * kernel[row_tap, col_tap]
        total = total + partial_row * masks[row_tap][:, None, None]
    return total

def reference(latents, timestep, label, time_table, class_table, dw_kernel, dw_bias, ln_gain, ln_bias, up_weight, up_bias, down_weight, down_bias, layer_scale):
    time_rows = time_table[timestep].astype(jnp.float32)
    class_rows = class_table[label].astype(jnp.float32)
    scale_full = layer_scale.astype(jnp.float32)
    direction = (class_rows * scale_full).astype(jnp.bfloat16)
    slope_image = lax.dot_general(direction, down_weight, (((1,), (1,)), ((), ())), preferred_element_type=jnp.float32)
    start_all = latents.astype(jnp.float32).reshape(IMGS, IH, W, C) + time_rows[:, None, None, :]
    kernel = dw_kernel.astype(jnp.float32)
    masks = jnp.ones((7, IH), jnp.float32)
    gain = ln_gain.astype(jnp.float32)
    shift = ln_bias.astype(jnp.float32)

    def one_image(items):
        start, class_vec, slope_vec = items
        padded = jnp.pad(start, ((3, 3), (3, 3), (0, 0)))
        mixed = stencil(padded, kernel, masks) + dw_bias.astype(jnp.float32)
        flat = mixed.reshape(IH * W, C)
        mean = lax.optimization_barrier(jnp.sum(flat, 1)) / C
        variance = lax.optimization_barrier(jnp.sum(flat * flat, 1)) / C - mean * mean
        inverse = lax.rsqrt(variance + EPSILON)
        normed = (flat - mean[:, None]) * inverse[:, None]
        scaled = (normed * gain + shift).astype(jnp.bfloat16)
        hidden = jnp.dot(scaled, up_weight, preferred_element_type=jnp.float32) + up_bias.astype(jnp.float32)
        active = gelu_tanh(hidden).astype(jnp.bfloat16)
        branch = jnp.dot(active, down_weight, preferred_element_type=jnp.float32) + down_bias.astype(jnp.float32)
        features = (start.reshape(IH * W, C) + scale_full * branch).astype(jnp.bfloat16)
        hidden_grad = (slope_vec[None, :] * gelu_slope(hidden)).astype(jnp.bfloat16)
        normed_grad = lax.dot_general(hidden_grad, up_weight, (((1,), (1,)), ((), ())), preferred_element_type=jnp.float32)
        gained = normed_grad * gain
        grad_first = lax.optimization_barrier(jnp.sum(gained, 1)) / C
        grad_second = lax.optimization_barrier(jnp.sum(gained * normed, 1)) / C
        mixed_grad = inverse[:, None] * (gained - grad_first[:, None] - normed * grad_second[:, None])
        grad_pad = jnp.pad(mixed_grad.reshape(IH, W, C), ((3, 3), (3, 3), (0, 0)))
        gradient = stencil(grad_pad, kernel[::-1, ::-1], masks) + class_vec[None, None, :]
        return (features.reshape(IH, W, C), gradient)
    features, gradient = lax.map(one_image, (start_all, class_rows, slope_image))
    return (features.reshape(H, W, C), gradient.reshape(H, W, C))
```

```python
import functools

import jax
import jax.numpy as jnp
from jax import lax
from jax.experimental import pallas as pl
from jax.experimental.pallas import tpu as pltpu
from jax.sharding import PartitionSpec as P

KAPPA = 0.7978845608028654
CUBIC = 0.044715
EPSILON = 1e-06
LANES = 128
MIB = 1 << 20


def call(body, outs, ins, scratch=(), limit=24, name=None, flops=0):
    specs = []
    args = []
    for item in ins:
        array, space = item if isinstance(item, tuple) else (item, pltpu.VMEM)
        specs.append(pl.BlockSpec(memory_space=space))
        args.append(array)
    return pl.pallas_call(
        body,
        out_shape=tuple(jax.ShapeDtypeStruct(s, d) for s, d in outs),
        in_specs=specs,
        out_specs=tuple(pl.BlockSpec(memory_space=pltpu.VMEM) for _ in outs),
        scratch_shapes=list(scratch),
        compiler_params=pltpu.CompilerParams(vmem_limit_bytes=limit * MIB),
        cost_estimate=pl.CostEstimate(flops=flops, transcendentals=0, bytes_accessed=0) if flops else None,
        name=name,
    )(*args)


def row_of(block, index):
    hit = lax.broadcasted_iota(jnp.int32, block.shape, 0) == index
    return jnp.sum(jnp.where(hit, block, 0.0), axis=0, keepdims=True)


def vec(ref):
    return ref[...].astype(jnp.float32).reshape(1, ref.shape[0])


def take(flat, first, count, stride):
    window = pl.ds(first, count, stride=stride) if stride > 1 else pl.ds(first, count)
    return jnp.concatenate([flat[l, window, :] for l in range(flat.shape[0])], axis=1)


def setup_kernel(
    timestep, label, time_table, class_table, layer_scale, down, time_out, class_out, slope_out, rows8, sems,
    *, images, half
):
    copies = []
    for i in range(images):
        base = pl.multiple_of((timestep[i] // 8) * 8, 8)
        copies.append(
            pltpu.make_async_copy(time_table.at[pl.ds(base, 8), :], rows8.at[i], sems.at[i])
        )
        copies[-1].start()
    mine = pl.multiple_of(lax.axis_index("chan") * half, half)
    scale = vec(layer_scale)
    table = class_table[...].astype(jnp.float32)
    table_half = class_table[:, pl.ds(mine, half)].astype(jnp.float32)
    full = [row_of(table, label[i]) for i in range(images)]
    for i in range(images):
        class_out[i : i + 1, :] = row_of(table_half, label[i])
    fill = [jnp.zeros_like(full[0])] * (8 - images)
    direction = (jnp.concatenate(full + fill, axis=0) * scale).astype(jnp.bfloat16)
    slope_out[...] = lax.dot_general(
        direction, down[...], (((1,), (1,)), ((), ())), preferred_element_type=jnp.float32
    )
    for i in range(images):
        copies[i].wait()
        time_out[i : i + 1, :] = row_of(rows8[i].astype(jnp.float32), timestep[i] % 8)


def stencil(cols, taps, store, flip, images, high, width):
    channels = cols.shape[2]
    row = lax.broadcasted_iota(jnp.int32, (high, LANES), 0)
    inside = [(row + (t - 3) >= 0) & (row + (t - 3) < high) for t in range(7)]
    for lane in range(0, channels, LANES):
        for image in range(images):
            first = image * high
            column = [cols[c, first : first + high, lane : lane + LANES] for c in range(width + 6)]
            total = [None] * width
            for t in range(7):
                part = [None] * width
                for d in range(7):
                    place = 8 * (6 - t) + 6 - d if flip else 8 * t + d
                    weight = jnp.broadcast_to(taps[place : place + 1, lane : lane + LANES], (high, LANES))
                    for c in range(width):
                        term = column[c + d] * weight
                        part[c] = term if d == 0 else part[c] + term
                for c in range(width):
                    moved = part[c]
                    if t != 3:
                        moved = pltpu.roll(moved, (3 - t) % high, 0)
                        moved = jnp.where(inside[t], moved, 0.0)
                    total[c] = moved if t == 0 else total[c] + moved
            for c in range(width):
                store(c, first, lane, total[c])


def load_taps(dw_kernel, taps):
    for t in range(7):
        taps[8 * t : 8 * t + 7, :] = dw_kernel[t].astype(jnp.float32)


def mix_kernel(
    own, left, right, time_rows, dw_kernel, dw_bias, gain, shift, mixed_out, start_out, flat, cols, taps,
    *, images, high, width
):
    rows = images * high
    position = lax.axis_index("rows")
    load_taps(dw_kernel, taps)
    for side, ref in enumerate((left, own, right)):
        for r in range(rows):
            cell = ref[r].astype(jnp.float32)
            for l in range(flat.shape[0]):
                flat[l, r * width : (r + 1) * width, :] = cell[:, l * LANES : (l + 1) * LANES]
        for c in range(width):
            place = (side - 1) * width + c + 3
            if place < 0 or place >= width + 6:
                continue
            for image in range(images):
                first = image * high
                value = take(flat, first * width + c, high, width) + time_rows[image : image + 1, :]
                if side == 0:
                    value = value * jnp.where(position > 0, 1.0, 0.0)
                if side == 2:
                    value = value * jnp.where(position < lax.axis_size("rows") - 1, 1.0, 0.0)
                cols[place, first : first + high, :] = value
                if side == 1:
                    start_out[c * rows + first : c * rows + first + high, :] = value
    bias = vec(dw_bias)

    def store(c, first, lane, value):
        mixed_out[c * rows + first : c * rows + first + high, lane : lane + LANES] = (
            value + bias[:, lane : lane + LANES]
        )

    stencil(cols, taps, store, False, images, high, width)
    tokens = rows * width
    mixed_out[tokens : tokens + 1, :] = vec(gain)
    mixed_out[tokens + 1 : tokens + 2, :] = vec(shift)


def mlp_kernel(
    own, other, slope, up, up_bias, down, branch_out, branch_send, grad_out, grad_send, sums_out, normed_out, inverse_out,
    active, hidden_grad, *, images, high, width, full, chunk
):
    tokens = images * high * width
    half = own.shape[1]
    hidden_size = up.shape[1]
    index = lax.axis_index("chan")
    mine = pl.multiple_of(index * half, half)
    theirs = pl.multiple_of((1 - index) * half, half)
    x = own[:tokens, :]
    y = other[:tokens, :]
    mean = (jnp.sum(x, 1, keepdims=True) + jnp.sum(y, 1, keepdims=True)) / full
    square = (jnp.sum(x * x, 1, keepdims=True) + jnp.sum(y * y, 1, keepdims=True)) / full
    inverse = lax.rsqrt(square - mean * mean + EPSILON)
    normed_x = (x - mean) * inverse
    normed_y = (y - mean) * inverse
    gain_x = own[tokens : tokens + 1, :]
    gain_y = other[tokens : tokens + 1, :]
    scaled_x = (normed_x * gain_x + own[tokens + 1 : tokens + 2, :]).astype(jnp.bfloat16)
    scaled_y = (normed_y * gain_y + other[tokens + 1 : tokens + 2, :]).astype(jnp.bfloat16)
    normed_out[...] = normed_x
    inverse_out[...] = jnp.broadcast_to(inverse, inverse_out.shape)
    bias = vec(up_bias)
    for j in range(0, hidden_size, chunk):
        hidden = jnp.dot(scaled_x, up[pl.ds(mine, half), j : j + chunk], preferred_element_type=jnp.float32)
        hidden = hidden + jnp.dot(
            scaled_y, up[pl.ds(theirs, half), j : j + chunk], preferred_element_type=jnp.float32
        )
        hidden = hidden + bias[:, j : j + chunk]
        cell = hidden * hidden
        tangent = jnp.tanh(KAPPA * (hidden + CUBIC * cell * hidden))
        grown = 0.5 * (1.0 + tangent)
        active[:, j : j + chunk] = (hidden * grown).astype(jnp.bfloat16)
        steep = grown + 0.5 * hidden * (1.0 - tangent * tangent) * KAPPA * (1.0 + 3.0 * CUBIC * cell)
        for c in range(width):
            for image in range(images):
                first = (c * images + image) * high
                hidden_grad[first : first + high, j : j + chunk] = (
                    slope[image : image + 1, j : j + chunk] * steep[first : first + high, :]
                ).astype(jnp.bfloat16)
    live = active[...]
    branch_send[...] = jnp.dot(live, down[:, pl.ds(theirs, half)], preferred_element_type=jnp.float32)
    branch_out[...] = jnp.dot(live, down[:, pl.ds(mine, half)], preferred_element_type=jnp.float32)
    back = hidden_grad[...]
    across = (((1,), (1,)), ((), ()))
    grad_y = lax.dot_general(back, up[pl.ds(theirs, half), :], across, preferred_element_type=jnp.float32)
    grad_x = lax.dot_general(back, up[pl.ds(mine, half), :], across, preferred_element_type=jnp.float32)
    grad_send[...] = grad_y.astype(jnp.bfloat16)
    grad_out[...] = grad_x
    gained_x = grad_x * gain_x
    gained_y = grad_y * gain_y
    first_sum = jnp.sum(gained_x, 1, keepdims=True) + jnp.sum(gained_y, 1, keepdims=True)
    second_sum = jnp.sum(gained_x * normed_x, 1, keepdims=True) + jnp.sum(gained_y * normed_y, 1, keepdims=True)
    lane = lax.broadcasted_iota(jnp.int32, (tokens, LANES), 1)
    sums_out[...] = jnp.where(lane == 0, first_sum, second_sum)


def join_kernel(
    branch, branch_other, start, down_bias, layer_scale, grad, grad_other, sums, sums_other, normed, inverse, gain,
    features_out, grad_out, tail_out, head_out, flat, *, rows, width, full
):
    tokens, half = branch.shape
    mine = pl.multiple_of(lax.axis_index("chan") * half, half)
    scale = layer_scale[pl.ds(mine, half)].astype(jnp.float32).reshape(1, half)
    features = start[...] + scale * (branch[...] + branch_other[...] + vec(down_bias))
    for c in range(width):
        for l in range(flat.shape[0]):
            flat[l, pl.ds(c, rows, stride=width), :] = features[
                c * rows : (c + 1) * rows, l * LANES : (l + 1) * LANES
            ]
    for r in range(rows):
        features_out[r] = take(flat, r * width, width, 1).astype(jnp.bfloat16)
    gained = (grad[...] + grad_other[...].astype(jnp.float32)) * vec(gain)
    both = sums[...] + sums_other[...]
    first_sum = both[:, 0:1] / full
    second_sum = both[:, 1:2] / full
    mixed_grad = inverse[:, 0:1] * (gained - first_sum - normed[...] * second_sum)
    grad_out[...] = mixed_grad
    short = mixed_grad.astype(jnp.bfloat16)
    edge = 3 * rows
    tail_out[...] = short[tokens - edge :, :]
    head_out[...] = short[:edge, :]


def unmix_kernel(own, left, right, class_rows, dw_kernel, gradient_out, flat, cols, taps, *, images, high, width):
    rows = images * high
    load_taps(dw_kernel, taps)
    for c in range(3):
        cols[c] = left[c * rows : (c + 1) * rows, :].astype(jnp.float32)
        cols[c + 3 + width] = right[c * rows : (c + 1) * rows, :].astype(jnp.float32)
    for c in range(width):
        cols[c + 3] = own[c * rows : (c + 1) * rows, :]
    classes = class_rows[...]

    def store(c, first, lane, value):
        image = first // high
        flat[lane // LANES, pl.ds(first * width + c, high, stride=width), :] = (
            value + classes[image : image + 1, lane : lane + LANES]
        )

    stencil(cols, taps, store, True, images, high, width)
    for r in range(rows):
        gradient_out[r] = take(flat, r * width, width, 1)


def neighbours(first, second, axis):
    count = lax.axis_size(axis)
    from_left = lax.ppermute(first, axis, [(i, i + 1) for i in range(count - 1)])
    from_right = lax.ppermute(second, axis, [(i + 1, i) for i in range(count - 1)])
    return from_left, from_right


def per_device(
    latents,
    timestep,
    label,
    time_table,
    class_table,
    dw_kernel,
    dw_bias,
    ln_gain,
    ln_bias,
    up_weight,
    up_bias,
    down_weight,
    down_bias,
    layer_scale,
):
    rows, width, half = latents.shape
    full = class_table.shape[1]
    images = timestep.shape[0]
    high = rows // images
    tokens = rows * width
    hidden_size = up_weight.shape[1]
    f32 = jnp.float32
    bf16 = jnp.bfloat16
    sizes = dict(images=images, high=high, width=width)
    swap = [(0, 1), (1, 0)]

    left, right = neighbours(latents, latents, "rows")
    time_rows, class_rows, slope = call(
        functools.partial(setup_kernel, images=images, half=half),
        [((8, half), f32), ((8, half), f32), ((8, hidden_size), f32)],
        [(timestep, pltpu.SMEM), (label, pltpu.SMEM), (time_table, pl.ANY), class_table, layer_scale, down_weight],
        [pltpu.VMEM((images, 8, half), bf16), pltpu.SemaphoreType.DMA((images,))],
        name="setup",
        flops=2 * 96 * full * hidden_size,
    )
    mixed, start = call(
        functools.partial(mix_kernel, **sizes),
        [((tokens + 8, half), f32), ((tokens, half), f32)],
        [latents, left, right, time_rows, dw_kernel, dw_bias, ln_gain, ln_bias],
        [
            pltpu.VMEM((half // LANES, tokens, LANES), f32),
            pltpu.VMEM((width + 6, rows, half), f32),
            pltpu.VMEM((56, half), f32),
        ],
        name="mix",
    )
    mixed_other = lax.ppermute(mixed, "chan", swap)
    branch, branch_send, grad, grad_send, sums, normed, inverse = call(
        functools.partial(mlp_kernel, full=full, chunk=512, **sizes),
        [
            ((tokens, half), f32),
            ((tokens, half), f32),
            ((tokens, half), f32),
            ((tokens, half), bf16),
            ((tokens, LANES), f32),
            ((tokens, half), f32),
            ((tokens, LANES), f32),
        ],
        [mixed, mixed_other, slope, up_weight, up_bias, down_weight],
        [pltpu.VMEM((tokens, hidden_size), bf16), pltpu.VMEM((tokens, hidden_size), bf16)],
        name="mlp",
        limit=40,
    )
    branch_other = lax.ppermute(branch_send, "chan", swap)
    grad_other = lax.ppermute(grad_send, "chan", swap)
    sums_other = lax.ppermute(sums, "chan", swap)
    features, mixed_grad, tail, head = call(
        functools.partial(join_kernel, rows=rows, width=width, full=full),
        [((rows, width, half), bf16), ((tokens, half), f32), ((3 * rows, half), bf16), ((3 * rows, half), bf16)],
        [
            branch, branch_other, start, down_bias, layer_scale,
            grad, grad_other, sums, sums_other, normed, inverse, ln_gain,
        ],
        [pltpu.VMEM((half // LANES, tokens, LANES), f32)],
        name="join",
    )
    features = lax.all_to_all(features, "rows", split_axis=0, concat_axis=1, tiled=True)
    left, right = neighbours(tail, head, "rows")
    (gradient,) = call(
        functools.partial(unmix_kernel, **sizes),
        [((rows, width, half), f32)],
        [mixed_grad, left, right, class_rows, dw_kernel],
        [
            pltpu.VMEM((half // LANES, tokens, LANES), f32),
            pltpu.VMEM((width + 6, rows, half), f32),
            pltpu.VMEM((56, half), f32),
        ],
        name="unmix",
    )
    return features, gradient


def solution(mesh):
    in_specs = (
        P("groups", "rows", "chan"),
        P("groups"),
        P("groups"),
        P(None, "chan"),
        P(),
        P(None, None, "chan"),
        P("chan"),
        P("chan"),
        P("chan"),
        P(None, "chan"),
        P("chan"),
        P("chan", None),
        P("chan"),
        P(),
    )
    out_specs = (P(("groups", "rows"), None, "chan"), P("groups", "rows", "chan"))
    return jax.shard_map(
        per_device, mesh=mesh, in_specs=in_specs, out_specs=out_specs, check_vma=False
    )
```

```python
import functools

import jax
import jax.numpy as jnp
from jax import lax
from jax.experimental import pallas as pl
from jax.experimental.pallas import tpu as pltpu
from jax.sharding import PartitionSpec as P

KAPPA = 0.7978845608028654
CUBIC = 0.044715
EPSILON = 1e-06
LANES = 128
MIB = 1 << 20


def call(body, outs, ins, scratch=(), limit=16, name=None, flops=0):
    specs = []
    args = []
    for item in ins:
        array, space = item if isinstance(item, tuple) else (item, pltpu.VMEM)
        specs.append(pl.BlockSpec(memory_space=space))
        if space == pltpu.HBM:
            array = pltpu.with_memory_space_constraint(array, pltpu.HBM)
        args.append(array)
    return pl.pallas_call(
        body,
        out_shape=tuple(jax.ShapeDtypeStruct(s, d) for s, d in outs),
        in_specs=specs,
        out_specs=tuple(pl.BlockSpec(memory_space=pltpu.VMEM) for _ in outs),
        scratch_shapes=list(scratch),
        compiler_params=pltpu.CompilerParams(vmem_limit_bytes=limit * MIB),
        cost_estimate=pl.CostEstimate(flops=flops, transcendentals=0, bytes_accessed=0) if flops else None,
        name=name,
    )(*args)


def row_of(block, index):
    hit = lax.broadcasted_iota(jnp.int32, block.shape, 0) == index
    return jnp.sum(jnp.where(hit, block, 0.0), axis=0, keepdims=True)


def vec(ref):
    return ref[...].astype(jnp.float32).reshape(1, ref.shape[0])


def take(flat, first, count, stride):
    window = pl.ds(first, count, stride=stride) if stride > 1 else pl.ds(first, count)
    return jnp.concatenate([flat[l, window, :] for l in range(flat.shape[0])], axis=1)


def setup_kernel(
    timestep, label, time_table, class_table, layer_scale, down, time_out, class_out, slope_out, down_out,
    step, kind, table, scale, rows8, sems, *, images, half
):
    pairs = ((timestep, step), (label, kind), (class_table, table), (layer_scale, scale), (down, down_out))
    copies = [pltpu.make_async_copy(a, b, sems.at[i]) for i, (a, b) in enumerate(pairs)]
    for copy in copies:
        copy.start()
    copies[0].wait()
    for i in range(images):
        base = pl.multiple_of((step[i] // 8) * 8, 8)
        copies.append(
            pltpu.make_async_copy(time_table.at[pl.ds(base, 8), :], rows8.at[i], sems.at[len(pairs) + i])
        )
        copies[-1].start()
    for copy in copies[1:4]:
        copy.wait()
    mine = pl.multiple_of(lax.axis_index("chan") * half, half)
    whole = table[...].astype(jnp.float32)
    part = table[:, pl.ds(mine, half)].astype(jnp.float32)
    full = [row_of(whole, kind[i]) for i in range(images)]
    for i in range(images):
        class_out[i : i + 1, :] = row_of(part, kind[i])
    fill = [jnp.zeros_like(full[0])] * (8 - images)
    direction = (jnp.concatenate(full + fill, axis=0) * vec(scale)).astype(jnp.bfloat16)
    for i in range(images):
        copies[len(pairs) + i].wait()
        time_out[i : i + 1, :] = row_of(rows8[i].astype(jnp.float32), step[i] % 8)
    copies[4].wait()
    slope_out[...] = lax.dot_general(
        direction, down_out[...], (((1,), (1,)), ((), ())), preferred_element_type=jnp.float32
    )


def stencil(cols, taps, store, flip, images, high, width):
    channels = cols.shape[2]
    row = lax.broadcasted_iota(jnp.int32, (high, LANES), 0)
    inside = [(row + (t - 3) >= 0) & (row + (t - 3) < high) for t in range(7)]
    for lane in range(0, channels, LANES):
        for image in range(images):
            first = image * high
            column = [cols[c, first : first + high, lane : lane + LANES] for c in range(width + 6)]
            total = [None] * width
            for t in range(7):
                part = [None] * width
                for d in range(7):
                    place = 8 * (6 - t) + 6 - d if flip else 8 * t + d
                    weight = jnp.broadcast_to(taps[place : place + 1, lane : lane + LANES], (high, LANES))
                    for c in range(width):
                        term = column[c + d] * weight
                        part[c] = term if d == 0 else part[c] + term
                for c in range(width):
                    moved = part[c]
                    if t != 3:
                        moved = pltpu.roll(moved, (3 - t) % high, 0)
                        moved = jnp.where(inside[t], moved, 0.0)
                    total[c] = moved if t == 0 else total[c] + moved
            for c in range(width):
                store(c, first, lane, total[c])


def load_taps(dw_kernel, taps):
    for t in range(7):
        taps[8 * t : 8 * t + 7, :] = dw_kernel[t].astype(jnp.float32)


def mix_kernel(
    own, left, right, time_rows, dw_kernel, dw_bias, gain, shift, mixed_out, start_out, flat, cols, taps,
    *, images, high, width
):
    rows = images * high
    position = lax.axis_index("rows")
    load_taps(dw_kernel, taps)
    for side, ref in enumerate((left, own, right)):
        for r in range(rows):
            cell = ref[r].astype(jnp.float32)
            for l in range(flat.shape[0]):
                flat[l, r * width : (r + 1) * width, :] = cell[:, l * LANES : (l + 1) * LANES]
        for c in range(width):
            place = (side - 1) * width + c + 3
            if place < 0 or place >= width + 6:
                continue
            for image in range(images):
                first = image * high
                value = take(flat, first * width + c, high, width) + time_rows[image : image + 1, :]
                if side == 0:
                    value = value * jnp.where(position > 0, 1.0, 0.0)
                if side == 2:
                    value = value * jnp.where(position < lax.axis_size("rows") - 1, 1.0, 0.0)
                cols[place, first : first + high, :] = value
                if side == 1:
                    start_out[c * rows + first : c * rows + first + high, :] = value
    bias = vec(dw_bias)

    def store(c, first, lane, value):
        mixed_out[c * rows + first : c * rows + first + high, lane : lane + LANES] = (
            value + bias[:, lane : lane + LANES]
        )

    stencil(cols, taps, store, False, images, high, width)
    tokens = rows * width
    mixed_out[tokens : tokens + 1, :] = vec(gain)
    mixed_out[tokens + 1 : tokens + 2, :] = vec(shift)


def forward_kernel(
    own, other, slope, up, up_bias, down, branch_out, branch_send, hidden_grad, normed_out, normed_other_out, inverse_out,
    active, *, images, high, width, full, chunk
):
    tokens = images * high * width
    half = own.shape[1]
    hidden_size = up.shape[1]
    index = lax.axis_index("chan")
    mine = pl.multiple_of(index * half, half)
    theirs = pl.multiple_of((1 - index) * half, half)
    x = own[:tokens, :]
    y = other[:tokens, :]
    mean = (jnp.sum(x, 1, keepdims=True) + jnp.sum(y, 1, keepdims=True)) / full
    square = (jnp.sum(x * x, 1, keepdims=True) + jnp.sum(y * y, 1, keepdims=True)) / full
    inverse = lax.rsqrt(square - mean * mean + EPSILON)
    normed_x = (x - mean) * inverse
    normed_y = (y - mean) * inverse
    scaled_x = normed_x * own[tokens : tokens + 1, :] + own[tokens + 1 : tokens + 2, :]
    scaled_y = normed_y * other[tokens : tokens + 1, :] + other[tokens + 1 : tokens + 2, :]
    scaled_x = scaled_x.astype(jnp.bfloat16)
    scaled_y = scaled_y.astype(jnp.bfloat16)
    normed_out[...] = normed_x
    normed_other_out[...] = normed_y
    inverse_out[...] = jnp.broadcast_to(inverse, inverse_out.shape)
    bias = vec(up_bias)
    for j in range(0, hidden_size, chunk):
        hidden = jnp.dot(scaled_x, up[pl.ds(mine, half), j : j + chunk], preferred_element_type=jnp.float32)
        hidden = hidden + jnp.dot(
            scaled_y, up[pl.ds(theirs, half), j : j + chunk], preferred_element_type=jnp.float32
        )
        hidden = hidden + bias[:, j : j + chunk]
        cell = hidden * hidden
        tangent = jnp.tanh(KAPPA * (hidden + CUBIC * cell * hidden))
        grown = 0.5 * (1.0 + tangent)
        active[:, j : j + chunk] = (hidden * grown).astype(jnp.bfloat16)
        steep = grown + 0.5 * hidden * (1.0 - tangent * tangent) * KAPPA * (1.0 + 3.0 * CUBIC * cell)
        for c in range(width):
            for image in range(images):
                first = (c * images + image) * high
                hidden_grad[first : first + high, j : j + chunk] = (
                    slope[image : image + 1, j : j + chunk] * steep[first : first + high, :]
                ).astype(jnp.bfloat16)
    live = active[...]
    branch_send[...] = jnp.dot(live, down[:, pl.ds(theirs, half)], preferred_element_type=jnp.float32)
    branch_out[...] = jnp.dot(live, down[:, pl.ds(mine, half)], preferred_element_type=jnp.float32)


def backward_kernel(
    hidden_grad, up, own, other, normed, normed_other, grad_out, grad_send, sums_out
):
    tokens, half = normed.shape
    index = lax.axis_index("chan")
    mine = pl.multiple_of(index * half, half)
    theirs = pl.multiple_of((1 - index) * half, half)
    back = hidden_grad[...]
    across = (((1,), (1,)), ((), ()))
    grad_y = lax.dot_general(back, up[pl.ds(theirs, half), :], across, preferred_element_type=jnp.float32)
    grad_x = lax.dot_general(back, up[pl.ds(mine, half), :], across, preferred_element_type=jnp.float32)
    grad_send[:, :half] = grad_y.astype(jnp.bfloat16)
    grad_out[...] = grad_x
    gained_x = grad_x * own[tokens : tokens + 1, :]
    gained_y = grad_y * other[tokens : tokens + 1, :]
    first_sum = jnp.sum(gained_x + gained_y, 1, keepdims=True)
    second_sum = jnp.sum(gained_x * normed[...] + gained_y * normed_other[...], 1, keepdims=True)
    lane = lax.broadcasted_iota(jnp.int32, (tokens, LANES), 1)
    sums = jnp.where(lane % 2 == 0, first_sum, second_sum)
    sums_out[...] = sums
    coarse = sums.astype(jnp.bfloat16).astype(jnp.float32)
    grad_send[:, half:] = jnp.where(lane < 2, coarse, sums - coarse).astype(jnp.bfloat16)


def features_kernel(branch, branch_other, start, down_bias, layer_scale, features_out, flat, *, rows, width):
    tokens, half = branch.shape
    mine = pl.multiple_of(lax.axis_index("chan") * half, half)
    scale = layer_scale[pl.ds(mine, half)].astype(jnp.float32).reshape(1, half)
    features = start[...] + scale * (branch[...] + branch_other[...] + vec(down_bias))
    for c in range(width):
        for l in range(flat.shape[0]):
            flat[l, pl.ds(c, rows, stride=width), :] = features[
                c * rows : (c + 1) * rows, l * LANES : (l + 1) * LANES
            ]
    for r in range(rows):
        features_out[r] = take(flat, r * width, width, 1).astype(jnp.bfloat16)


def norm_grad_kernel(
    grad, grad_other, sums, normed, inverse, gain, grad_out, inner_out, outer_out, *, rows, full
):
    tokens, half = grad.shape
    gained = (grad[...] + grad_other[:, :half].astype(jnp.float32)) * vec(gain)
    extra = grad_other[:, half:].astype(jnp.float32)
    first_sum = (sums[:, 0:1] + (extra[:, 0:1] + extra[:, 2:3])) / full
    second_sum = (sums[:, 1:2] + (extra[:, 1:2] + extra[:, 3:4])) / full
    grad_out[...] = inverse[:, 0:1] * (gained - first_sum - normed[...] * second_sum)
    edge = 3 * rows
    parity = lax.axis_index("rows") % 2
    low = pl.multiple_of(parity * (tokens - edge), 8)
    high = pl.multiple_of((1 - parity) * (tokens - edge), 8)
    inner_out[...] = grad_out[pl.ds(high, edge), :].astype(jnp.bfloat16)
    outer_out[...] = grad_out[pl.ds(low, edge), :].astype(jnp.bfloat16)


def unmix_kernel(own, inner, outer, class_rows, dw_kernel, gradient_out, flat, cols, taps, *, images, high, width):
    rows = images * high
    load_taps(dw_kernel, taps)
    position = lax.axis_index("rows")
    parity = position % 2
    within = (position > 0) & (position < lax.axis_size("rows") - 1)
    inner_side = pl.multiple_of((1 - parity) * (3 + width), 1)
    outer_side = pl.multiple_of(parity * (3 + width), 1)
    for c in range(3):
        cols[inner_side + c] = inner[c * rows : (c + 1) * rows, :].astype(jnp.float32)
        cols[outer_side + c] = outer[c * rows : (c + 1) * rows, :].astype(jnp.float32) * jnp.where(within, 1.0, 0.0)
    for c in range(width):
        cols[c + 3] = own[c * rows : (c + 1) * rows, :]
    classes = class_rows[...]

    def store(c, first, lane, value):
        image = first // high
        flat[lane // LANES, pl.ds(first * width + c, high, stride=width), :] = (
            value + classes[image : image + 1, lane : lane + LANES]
        )

    stencil(cols, taps, store, True, images, high, width)
    for r in range(rows):
        gradient_out[r] = take(flat, r * width, width, 1)


def neighbours(first, second, axis):
    count = lax.axis_size(axis)
    from_left = lax.ppermute(first, axis, [(i, i + 1) for i in range(count - 1)])
    from_right = lax.ppermute(second, axis, [(i + 1, i) for i in range(count - 1)])
    return from_left, from_right


def per_device(
    latents,
    timestep,
    label,
    time_table,
    class_table,
    dw_kernel,
    dw_bias,
    ln_gain,
    ln_bias,
    up_weight,
    up_bias,
    down_weight,
    down_bias,
    layer_scale,
):
    rows, width, half = latents.shape
    full = class_table.shape[1]
    images = timestep.shape[0]
    high = rows // images
    tokens = rows * width
    hidden_size = up_weight.shape[1]
    f32 = jnp.float32
    bf16 = jnp.bfloat16
    sizes = dict(images=images, high=high, width=width)
    swap = [(0, 1), (1, 0)]

    left, right = neighbours(latents, latents, "rows")
    time_rows, class_rows, slope, down = call(
        functools.partial(setup_kernel, images=images, half=half),
        [((8, half), f32), ((8, half), f32), ((8, hidden_size), f32), (down_weight.shape, bf16)],
        [(a, pltpu.HBM) for a in (timestep, label, time_table, class_table, layer_scale, down_weight)],
        [
            pltpu.SMEM(timestep.shape, jnp.int32),
            pltpu.SMEM(label.shape, jnp.int32),
            pltpu.VMEM(class_table.shape, bf16),
            pltpu.VMEM(layer_scale.shape, bf16),
            pltpu.VMEM((images, 8, half), bf16),
            pltpu.SemaphoreType.DMA((5 + images,)),
        ],
        name="setup",
        flops=2 * 96 * full * hidden_size,
    )
    mixed, start = call(
        functools.partial(mix_kernel, **sizes),
        [((tokens + 8, half), f32), ((tokens, half), f32)],
        [latents, left, right, time_rows, dw_kernel, dw_bias, ln_gain, ln_bias],
        [
            pltpu.VMEM((half // LANES, tokens, LANES), f32),
            pltpu.VMEM((width + 6, rows, half), f32),
            pltpu.VMEM((56, half), f32),
        ],
        name="mix",
    )
    mixed_other = lax.ppermute(mixed, "chan", swap)
    branch, branch_send, hidden_grad, normed, normed_other, inverse = call(
        functools.partial(forward_kernel, full=full, chunk=512, **sizes),
        [
            ((tokens, half), f32),
            ((tokens, half), f32),
            ((tokens, hidden_size), bf16),
            ((tokens, half), f32),
            ((tokens, half), f32),
            ((tokens, LANES), f32),
        ],
        [mixed, mixed_other, slope, up_weight, up_bias, down],
        [pltpu.VMEM((tokens, hidden_size), bf16)],
        name="forward",
    )
    branch_other = lax.ppermute(branch_send, "chan", swap)
    grad, grad_send, sums = call(
        backward_kernel,
        [((tokens, half), f32), ((tokens, half + LANES), bf16), ((tokens, LANES), f32)],
        [hidden_grad, up_weight, mixed, mixed_other, normed, normed_other],
        name="backward",
    )
    grad_other = lax.ppermute(grad_send, "chan", swap)
    (features,) = call(
        functools.partial(features_kernel, rows=rows, width=width),
        [((rows, width, half), bf16)],
        [branch, branch_other, start, down_bias, layer_scale],
        [pltpu.VMEM((half // LANES, tokens, LANES), f32)],
        name="join",
    )
    features = lax.all_to_all(features, "rows", split_axis=0, concat_axis=1, tiled=True)
    mixed_grad, inner, outer = call(
        functools.partial(norm_grad_kernel, rows=rows, full=full),
        [((tokens, half), f32), ((3 * rows, half), bf16), ((3 * rows, half), bf16)],
        [grad, grad_other, sums, normed, inverse, ln_gain],
        name="norm_grad",
    )
    count = lax.axis_size("rows")
    inner = lax.ppermute(inner, "rows", [(i, i ^ 1) for i in range(count)])
    outer = lax.ppermute(outer, "rows", [(i, min(max((i + 1 ^ 1) - 1, 0), count - 1)) for i in range(count)])
    (gradient,) = call(
        functools.partial(unmix_kernel, **sizes),
        [((rows, width, half), f32)],
        [mixed_grad, inner, outer, class_rows, dw_kernel],
        [
            pltpu.VMEM((half // LANES, tokens, LANES), f32),
            pltpu.VMEM((width + 6, rows, half), f32),
            pltpu.VMEM((56, half), f32),
        ],
        name="unmix",
    )
    return features, gradient


def solution(mesh):
    in_specs = (
        P("groups", "rows", "chan"),
        P("groups"),
        P("groups"),
        P(None, "chan"),
        P(),
        P(None, None, "chan"),
        P("chan"),
        P("chan"),
        P("chan"),
        P(None, "chan"),
        P("chan"),
        P("chan", None),
        P("chan"),
        P(),
    )
    out_specs = (P(("groups", "rows"), None, "chan"), P("groups", "rows", "chan"))
    return jax.shard_map(
        per_device, mesh=mesh, in_specs=in_specs, out_specs=out_specs, check_vma=False
    )
```

```python
import functools

import jax
import jax.numpy as jnp
from jax import lax
from jax.experimental import pallas as pl
from jax.experimental.pallas import tpu as pltpu
from jax.sharding import PartitionSpec as P

KAPPA = 0.7978845608028654
CUBIC = 0.044715
EPSILON = 1e-06
LANES = 128
MIB = 1 << 20


def call(body, outs, ins, scratch=(), limit=16, name=None, flops=0):
    specs = []
    args = []
    for item in ins:
        array, space = item if isinstance(item, tuple) else (item, pltpu.VMEM)
        specs.append(pl.BlockSpec(memory_space=space))
        if space == pltpu.HBM:
            array = pltpu.with_memory_space_constraint(array, pltpu.HBM)
        args.append(array)
    return pl.pallas_call(
        body,
        out_shape=tuple(jax.ShapeDtypeStruct(s, d) for s, d in outs),
        in_specs=specs,
        out_specs=tuple(pl.BlockSpec(memory_space=pltpu.VMEM) for _ in outs),
        scratch_shapes=list(scratch),
        compiler_params=pltpu.CompilerParams(vmem_limit_bytes=limit * MIB),
        cost_estimate=pl.CostEstimate(flops=flops, transcendentals=0, bytes_accessed=0) if flops else None,
        name=name,
    )(*args)


def row_of(block, index):
    hit = lax.broadcasted_iota(jnp.int32, block.shape, 0) == index
    return jnp.sum(jnp.where(hit, block, 0.0), axis=0, keepdims=True)


def vec(ref):
    return ref[...].astype(jnp.float32).reshape(1, ref.shape[0])


def take(flat, first, count, stride):
    window = pl.ds(first, count, stride=stride) if stride > 1 else pl.ds(first, count)
    return jnp.concatenate([flat[l, window, :] for l in range(flat.shape[0])], axis=1)


def setup_kernel(
    timestep, label, time_table, class_table, layer_scale, down, time_out, class_out, direction_out, down_out,
    step, kind, table, scale, rows8, sems, *, images, half
):
    pairs = ((timestep, step), (label, kind), (class_table, table), (layer_scale, scale), (down, down_out))
    copies = [pltpu.make_async_copy(a, b, sems.at[i]) for i, (a, b) in enumerate(pairs)]
    for copy in copies:
        copy.start()
    copies[0].wait()
    for i in range(images):
        base = pl.multiple_of((step[i] // 8) * 8, 8)
        copies.append(
            pltpu.make_async_copy(time_table.at[pl.ds(base, 8), :], rows8.at[i], sems.at[len(pairs) + i])
        )
        copies[-1].start()
    for copy in copies[1:4]:
        copy.wait()
    mine = pl.multiple_of(lax.axis_index("chan") * half, half)
    whole = table[...].astype(jnp.float32)
    part = table[:, pl.ds(mine, half)].astype(jnp.float32)
    full = [row_of(whole, kind[i]) for i in range(images)]
    for i in range(images):
        class_out[i : i + 1, :] = row_of(part, kind[i])
    fill = [jnp.zeros_like(full[0])] * (8 - images)
    direction_out[...] = (jnp.concatenate(full + fill, axis=0) * vec(scale)).astype(jnp.bfloat16)
    for i in range(images):
        copies[len(pairs) + i].wait()
        time_out[i : i + 1, :] = row_of(rows8[i].astype(jnp.float32), step[i] % 8)
    copies[4].wait()


def slope_kernel(direction, down, slope_out):
    slope_out[...] = lax.dot_general(
        direction[...], down[...], (((1,), (1,)), ((), ())), preferred_element_type=jnp.float32
    )


def stencil(cols, taps, store, flip, images, high, width):
    channels = cols.shape[2]
    row = lax.broadcasted_iota(jnp.int32, (high, LANES), 0)
    inside = [(row + (t - 3) >= 0) & (row + (t - 3) < high) for t in range(7)]
    for lane in range(0, channels, LANES):
        for image in range(images):
            first = image * high
            column = [cols[c, first : first + high, lane : lane + LANES] for c in range(width + 6)]
            total = [None] * width
            for t in range(7):
                part = [None] * width
                for d in range(7):
                    place = 8 * (6 - t) + 6 - d if flip else 8 * t + d
                    weight = jnp.broadcast_to(taps[place : place + 1, lane : lane + LANES], (high, LANES))
                    for c in range(width):
                        term = column[c + d] * weight
                        part[c] = term if d == 0 else part[c] + term
                for c in range(width):
                    moved = part[c]
                    if t != 3:
                        moved = pltpu.roll(moved, (3 - t) % high, 0)
                        moved = jnp.where(inside[t], moved, 0.0)
                    total[c] = moved if t == 0 else total[c] + moved
            for c in range(width):
                store(c, first, lane, total[c])


def load_taps(dw_kernel, taps):
    for t in range(7):
        taps[8 * t : 8 * t + 7, :] = dw_kernel[t].astype(jnp.float32)


def mix_kernel(
    own, inner, outer, time_rows, dw_kernel, dw_bias, gain, shift, mixed_out, start_out, flat, cols, taps,
    *, images, high, width
):
    rows = images * high
    position = lax.axis_index("rows")
    odd = position % 2 == 1
    load_taps(dw_kernel, taps)
    for side in range(3):
        for r in range(rows):
            if side == 1:
                cell = own[r].astype(jnp.float32)
            else:
                near = inner[r].astype(jnp.float32)
                far = outer[r].astype(jnp.float32)
                cell = jnp.where(odd, near, far) if side == 0 else jnp.where(odd, far, near)
            for l in range(flat.shape[0]):
                flat[l, r * width : (r + 1) * width, :] = cell[:, l * LANES : (l + 1) * LANES]
        for c in range(width):
            place = (side - 1) * width + c + 3
            if place < 0 or place >= width + 6:
                continue
            for image in range(images):
                first = image * high
                value = take(flat, first * width + c, high, width) + time_rows[image : image + 1, :]
                if side == 0:
                    value = value * jnp.where(position > 0, 1.0, 0.0)
                if side == 2:
                    value = value * jnp.where(position < lax.axis_size("rows") - 1, 1.0, 0.0)
                cols[place, first : first + high, :] = value
                if side == 1:
                    start_out[c * rows + first : c * rows + first + high, :] = value
    bias = vec(dw_bias)

    def store(c, first, lane, value):
        mixed_out[c * rows + first : c * rows + first + high, lane : lane + LANES] = (
            value + bias[:, lane : lane + LANES]
        )

    stencil(cols, taps, store, False, images, high, width)
    tokens = rows * width
    mixed_out[tokens : tokens + 1, :] = vec(gain)
    mixed_out[tokens + 1 : tokens + 2, :] = vec(shift)


def forward_kernel(
    own, other, slope, up, up_bias, down, branch_out, branch_send, hidden_grad, normed_out, normed_other_out, inverse_out,
    active, *, images, high, width, full, chunk
):
    tokens = images * high * width
    half = own.shape[1]
    hidden_size = up.shape[1]
    index = lax.axis_index("chan")
    mine = pl.multiple_of(index * half, half)
    theirs = pl.multiple_of((1 - index) * half, half)
    x = own[:tokens, :]
    y = other[:tokens, :]
    mean = (jnp.sum(x, 1, keepdims=True) + jnp.sum(y, 1, keepdims=True)) / full
    square = (jnp.sum(x * x, 1, keepdims=True) + jnp.sum(y * y, 1, keepdims=True)) / full
    inverse = lax.rsqrt(square - mean * mean + EPSILON)
    normed_x = (x - mean) * inverse
    normed_y = (y - mean) * inverse
    scaled_x = normed_x * own[tokens : tokens + 1, :] + own[tokens + 1 : tokens + 2, :]
    scaled_y = normed_y * other[tokens : tokens + 1, :] + other[tokens + 1 : tokens + 2, :]
    scaled_x = scaled_x.astype(jnp.bfloat16)
    scaled_y = scaled_y.astype(jnp.bfloat16)
    normed_out[...] = normed_x
    normed_other_out[...] = normed_y
    inverse_out[...] = jnp.broadcast_to(inverse, inverse_out.shape)
    bias = vec(up_bias)
    for j in range(0, hidden_size, chunk):
        hidden = jnp.dot(scaled_x, up[pl.ds(mine, half), j : j + chunk], preferred_element_type=jnp.float32)
        hidden = hidden + jnp.dot(
            scaled_y, up[pl.ds(theirs, half), j : j + chunk], preferred_element_type=jnp.float32
        )
        hidden = hidden + bias[:, j : j + chunk]
        cell = hidden * hidden
        tangent = jnp.tanh(KAPPA * (hidden + CUBIC * cell * hidden))
        grown = 0.5 * (1.0 + tangent)
        active[:, j : j + chunk] = (hidden * grown).astype(jnp.bfloat16)
        steep = grown + 0.5 * hidden * (1.0 - tangent * tangent) * KAPPA * (1.0 + 3.0 * CUBIC * cell)
        for c in range(width):
            for image in range(images):
                first = (c * images + image) * high
                hidden_grad[first : first + high, j : j + chunk] = (
                    slope[image : image + 1, j : j + chunk] * steep[first : first + high, :]
                ).astype(jnp.bfloat16)
    live = active[...]
    branch_send[...] = jnp.dot(live, down[:, pl.ds(theirs, half)], preferred_element_type=jnp.float32)
    branch_out[...] = jnp.dot(live, down[:, pl.ds(mine, half)], preferred_element_type=jnp.float32)


def backward_kernel(
    hidden_grad, up, own, other, normed, normed_other, grad_out, grad_send, sums_out
):
    tokens, half = normed.shape
    index = lax.axis_index("chan")
    mine = pl.multiple_of(index * half, half)
    theirs = pl.multiple_of((1 - index) * half, half)
    back = hidden_grad[...]
    across = (((1,), (1,)), ((), ()))
    grad_y = lax.dot_general(back, up[pl.ds(theirs, half), :], across, preferred_element_type=jnp.float32)
    grad_x = lax.dot_general(back, up[pl.ds(mine, half), :], across, preferred_element_type=jnp.float32)
    grad_send[:, :half] = grad_y.astype(jnp.bfloat16)
    grad_out[...] = grad_x
    gained_x = grad_x * own[tokens : tokens + 1, :]
    gained_y = grad_y * other[tokens : tokens + 1, :]
    first_sum = jnp.sum(gained_x + gained_y, 1, keepdims=True)
    second_sum = jnp.sum(gained_x * normed[...] + gained_y * normed_other[...], 1, keepdims=True)
    lane = lax.broadcasted_iota(jnp.int32, (tokens, LANES), 1)
    sums = jnp.where(lane % 2 == 0, first_sum, second_sum)
    sums_out[...] = sums
    coarse = sums.astype(jnp.bfloat16).astype(jnp.float32)
    grad_send[:, half:] = jnp.where(lane < 2, coarse, sums - coarse).astype(jnp.bfloat16)


def features_kernel(branch, branch_other, start, down_bias, layer_scale, features_out, flat, *, rows, width):
    tokens, half = branch.shape
    mine = pl.multiple_of(lax.axis_index("chan") * half, half)
    scale = layer_scale[pl.ds(mine, half)].astype(jnp.float32).reshape(1, half)
    features = start[...] + scale * (branch[...] + branch_other[...] + vec(down_bias))
    for c in range(width):
        for l in range(flat.shape[0]):
            flat[l, pl.ds(c, rows, stride=width), :] = features[
                c * rows : (c + 1) * rows, l * LANES : (l + 1) * LANES
            ]
    for r in range(rows):
        features_out[r] = take(flat, r * width, width, 1).astype(jnp.bfloat16)


def norm_grad_kernel(
    grad, grad_other, sums, normed, inverse, gain, grad_out, inner_out, outer_out, *, rows, full
):
    tokens, half = grad.shape
    gained = (grad[...] + grad_other[:, :half].astype(jnp.float32)) * vec(gain)
    extra = grad_other[:, half:].astype(jnp.float32)
    first_sum = (sums[:, 0:1] + (extra[:, 0:1] + extra[:, 2:3])) / full
    second_sum = (sums[:, 1:2] + (extra[:, 1:2] + extra[:, 3:4])) / full
    grad_out[...] = inverse[:, 0:1] * (gained - first_sum - normed[...] * second_sum)
    edge = 3 * rows
    parity = lax.axis_index("rows") % 2
    low = pl.multiple_of(parity * (tokens - edge), 8)
    high = pl.multiple_of((1 - parity) * (tokens - edge), 8)
    inner_out[...] = grad_out[pl.ds(high, edge), :].astype(jnp.bfloat16)
    outer_out[...] = grad_out[pl.ds(low, edge), :].astype(jnp.bfloat16)


def unmix_kernel(own, inner, outer, class_rows, dw_kernel, gradient_out, flat, cols, taps, *, images, high, width):
    rows = images * high
    load_taps(dw_kernel, taps)
    position = lax.axis_index("rows")
    parity = position % 2
    within = (position > 0) & (position < lax.axis_size("rows") - 1)
    inner_side = pl.multiple_of((1 - parity) * (3 + width), 1)
    outer_side = pl.multiple_of(parity * (3 + width), 1)
    for c in range(3):
        cols[inner_side + c] = inner[c * rows : (c + 1) * rows, :].astype(jnp.float32)
        cols[outer_side + c] = outer[c * rows : (c + 1) * rows, :].astype(jnp.float32) * jnp.where(within, 1.0, 0.0)
    for c in range(width):
        cols[c + 3] = own[c * rows : (c + 1) * rows, :]
    classes = class_rows[...]

    def store(c, first, lane, value):
        image = first // high
        flat[lane // LANES, pl.ds(first * width + c, high, stride=width), :] = (
            value + classes[image : image + 1, lane : lane + LANES]
        )

    stencil(cols, taps, store, True, images, high, width)
    for r in range(rows):
        gradient_out[r] = take(flat, r * width, width, 1)


def pair_exchange(inner, outer, axis):
    count = lax.axis_size(axis)
    with jax.named_scope("inner"):
        inner = lax.ppermute(inner, axis, [(i, i ^ 1) for i in range(count)])
    with jax.named_scope("outer"):
        outer = lax.ppermute(
            outer, axis, [(i, min(max(((i + 1) ^ 1) - 1, 0), count - 1)) for i in range(count)]
        )
    return inner, outer


def per_device(
    latents,
    timestep,
    label,
    time_table,
    class_table,
    dw_kernel,
    dw_bias,
    ln_gain,
    ln_bias,
    up_weight,
    up_bias,
    down_weight,
    down_bias,
    layer_scale,
):
    rows, width, half = latents.shape
    full = class_table.shape[1]
    images = timestep.shape[0]
    high = rows // images
    tokens = rows * width
    hidden_size = up_weight.shape[1]
    f32 = jnp.float32
    bf16 = jnp.bfloat16
    sizes = dict(images=images, high=high, width=width)
    swap = [(0, 1), (1, 0)]

    with jax.named_scope("latent_halo"):
        inner, outer = pair_exchange(latents, latents, "rows")
    time_rows, class_rows, direction, down = call(
        functools.partial(setup_kernel, images=images, half=half),
        [((8, half), f32), ((8, half), f32), ((8, full), bf16), (down_weight.shape, bf16)],
        [(a, pltpu.HBM) for a in (timestep, label, time_table, class_table, layer_scale, down_weight)],
        [
            pltpu.SMEM(timestep.shape, jnp.int32),
            pltpu.SMEM(label.shape, jnp.int32),
            pltpu.VMEM(class_table.shape, bf16),
            pltpu.VMEM(layer_scale.shape, bf16),
            pltpu.VMEM((images, 8, half), bf16),
            pltpu.SemaphoreType.DMA((5 + images,)),
        ],
        name="setup",
    )
    mixed, start = call(
        functools.partial(mix_kernel, **sizes),
        [((tokens + 8, half), f32), ((tokens, half), f32)],
        [latents, inner, outer, time_rows, dw_kernel, dw_bias, ln_gain, ln_bias],
        [
            pltpu.VMEM((half // LANES, tokens, LANES), f32),
            pltpu.VMEM((width + 6, rows, half), f32),
            pltpu.VMEM((56, half), f32),
        ],
        name="mix",
    )
    mixed_other = lax.ppermute(mixed, "chan", swap)
    direction, _ = lax.optimization_barrier((direction, mixed))
    (slope,) = call(slope_kernel, [((8, hidden_size), f32)], [direction, down], name="slope")
    branch, branch_send, hidden_grad, normed, normed_other, inverse = call(
        functools.partial(forward_kernel, full=full, chunk=512, **sizes),
        [
            ((tokens, half), f32),
            ((tokens, half), f32),
            ((tokens, hidden_size), bf16),
            ((tokens, half), f32),
            ((tokens, half), f32),
            ((tokens, LANES), f32),
        ],
        [mixed, mixed_other, slope, up_weight, up_bias, down],
        [pltpu.VMEM((tokens, hidden_size), bf16)],
        name="forward",
    )
    branch_other = lax.ppermute(branch_send, "chan", swap)
    grad, grad_send, sums = call(
        backward_kernel,
        [((tokens, half), f32), ((tokens, half + LANES), bf16), ((tokens, LANES), f32)],
        [hidden_grad, up_weight, mixed, mixed_other, normed, normed_other],
        name="backward",
    )
    grad_other = lax.ppermute(grad_send, "chan", swap)
    (features,) = call(
        functools.partial(features_kernel, rows=rows, width=width),
        [((rows, width, half), bf16)],
        [branch, branch_other, start, down_bias, layer_scale],
        [pltpu.VMEM((half // LANES, tokens, LANES), f32)],
        name="join",
    )
    with jax.named_scope("spread"):
        features = lax.all_to_all(features, "rows", split_axis=0, concat_axis=1, tiled=True)
    mixed_grad, inner, outer = call(
        functools.partial(norm_grad_kernel, rows=rows, full=full),
        [((tokens, half), f32), ((3 * rows, half), bf16), ((3 * rows, half), bf16)],
        [grad, grad_other, sums, normed, inverse, ln_gain],
        name="norm_grad",
    )
    with jax.named_scope("grad_halo"):
        inner, outer = pair_exchange(inner, outer, "rows")
    (gradient,) = call(
        functools.partial(unmix_kernel, **sizes),
        [((rows, width, half), f32)],
        [mixed_grad, inner, outer, class_rows, dw_kernel],
        [
            pltpu.VMEM((half // LANES, tokens, LANES), f32),
            pltpu.VMEM((width + 6, rows, half), f32),
            pltpu.VMEM((56, half), f32),
        ],
        name="unmix",
    )
    return features, gradient


def solution(mesh):
    in_specs = (
        P("groups", "rows", "chan"),
        P("groups"),
        P("groups"),
        P(None, "chan"),
        P(),
        P(None, None, "chan"),
        P("chan"),
        P("chan"),
        P("chan"),
        P(None, "chan"),
        P("chan"),
        P("chan", None),
        P("chan"),
        P(),
    )
    out_specs = (P(("groups", "rows"), None, "chan"), P("groups", "rows", "chan"))
    return jax.shard_map(
        per_device, mesh=mesh, in_specs=in_specs, out_specs=out_specs, check_vma=False
    )
```

```python
import functools

import jax
import jax.numpy as jnp
from jax import lax
from jax.experimental import pallas as pl
from jax.experimental.pallas import tpu as pltpu
from jax.sharding import PartitionSpec as P

KAPPA = 0.7978845608028654
CUBIC = 0.044715
EPSILON = 1e-06
LANES = 128
MIB = 1 << 20


def call(body, outs, ins, scratch=(), limit=16, name=None, flops=0):
    specs = []
    args = []
    for item in ins:
        array, space = item if isinstance(item, tuple) else (item, pltpu.VMEM)
        specs.append(pl.BlockSpec(memory_space=space))
        if space == pltpu.HBM:
            array = pltpu.with_memory_space_constraint(array, pltpu.HBM)
        args.append(array)
    return pl.pallas_call(
        body,
        out_shape=tuple(jax.ShapeDtypeStruct(s, d) for s, d in outs),
        in_specs=specs,
        out_specs=tuple(pl.BlockSpec(memory_space=pltpu.VMEM) for _ in outs),
        scratch_shapes=list(scratch),
        compiler_params=pltpu.CompilerParams(vmem_limit_bytes=limit * MIB),
        cost_estimate=pl.CostEstimate(flops=flops, transcendentals=0, bytes_accessed=0) if flops else None,
        name=name,
    )(*args)


def row_of(block, index):
    hit = lax.broadcasted_iota(jnp.int32, block.shape, 0) == index
    return jnp.sum(jnp.where(hit, block, 0.0), axis=0, keepdims=True)


def vec(ref):
    return ref[...].astype(jnp.float32).reshape(1, ref.shape[0])


def take(flat, first, count, stride):
    window = pl.ds(first, count, stride=stride) if stride > 1 else pl.ds(first, count)
    return jnp.concatenate([flat[l, window, :] for l in range(flat.shape[0])], axis=1)


def setup_kernel(
    timestep, label, time_table, class_table, layer_scale, down, time_out, class_out, direction_out, down_out,
    step, kind, table, scale, rows8, sems, *, images, half
):
    pairs = ((timestep, step), (label, kind), (class_table, table), (layer_scale, scale), (down, down_out))
    copies = [pltpu.make_async_copy(a, b, sems.at[i]) for i, (a, b) in enumerate(pairs)]
    for copy in copies:
        copy.start()
    copies[0].wait()
    for i in range(images):
        base = pl.multiple_of((step[i] // 8) * 8, 8)
        copies.append(
            pltpu.make_async_copy(time_table.at[pl.ds(base, 8), :], rows8.at[i], sems.at[len(pairs) + i])
        )
        copies[-1].start()
    for copy in copies[1:4]:
        copy.wait()
    mine = pl.multiple_of(lax.axis_index("chan") * half, half)
    whole = table[...].astype(jnp.float32)
    part = table[:, pl.ds(mine, half)].astype(jnp.float32)
    full = [row_of(whole, kind[i]) for i in range(images)]
    for i in range(images):
        class_out[i : i + 1, :] = row_of(part, kind[i])
    fill = [jnp.zeros_like(full[0])] * (8 - images)
    direction_out[...] = (jnp.concatenate(full + fill, axis=0) * vec(scale)).astype(jnp.bfloat16)
    for i in range(images):
        copies[len(pairs) + i].wait()
        time_out[i : i + 1, :] = row_of(rows8[i].astype(jnp.float32), step[i] % 8)
    copies[4].wait()


def slope_kernel(direction, down, slope_out):
    slope_out[...] = lax.dot_general(
        direction[...], down[...], (((1,), (1,)), ((), ())), preferred_element_type=jnp.float32
    )


def stencil(cols, places, taps, base, store, flip, images, high, width):
    channels = cols.shape[2]
    row = lax.broadcasted_iota(jnp.int32, (high, LANES), 0)
    inside = [(row + (t - 3) >= 0) & (row + (t - 3) < high) for t in range(7)]
    for lane in range(0, channels, LANES):
        for image in range(images):
            first = image * high
            column = {p: cols[i, first : first + high, lane : lane + LANES] for i, p in enumerate(places)}
            total = [base(c, first, lane) for c in range(width)]
            for t in range(7):
                part = [None] * width
                for d in range(7):
                    place = 8 * (6 - t) + 6 - d if flip else 8 * t + d
                    weight = jnp.broadcast_to(taps[place : place + 1, lane : lane + LANES], (high, LANES))
                    for c in range(width):
                        if c + d in column:
                            term = column[c + d] * weight
                            part[c] = term if part[c] is None else part[c] + term
                for c in range(width):
                    moved = part[c]
                    if moved is None:
                        continue
                    if t != 3:
                        moved = pltpu.roll(moved, (3 - t) % high, 0)
                        moved = jnp.where(inside[t], moved, 0.0)
                    total[c] = total[c] + moved
            for c in range(width):
                store(c, first, lane, total[c])


def own_places(width):
    return tuple(range(3, 3 + width))


def side_places(width):
    return (0, 1, 2, 3 + width, 4 + width, 5 + width)


def writer(out, rows):
    def store(c, first, lane, value):
        out[c * rows + first : c * rows + first + value.shape[0], lane : lane + LANES] = value

    return store


def reader(ref, rows, high):
    return lambda c, first, lane: ref[c * rows + first : c * rows + first + high, lane : lane + LANES]


def unpack(tile, flat, rows, width):
    for r in range(rows):
        cell = tile(r)
        for l in range(flat.shape[0]):
            flat[l, r * width : (r + 1) * width, :] = cell[:, l * LANES : (l + 1) * LANES]


def mix_own_kernel(own, time_rows, dw_kernel, dw_bias, part_out, start_out, taps, flat, cols, *, images, high, width):
    rows = images * high
    for t in range(7):
        taps[8 * t : 8 * t + 7, :] = dw_kernel[t].astype(jnp.float32)
    unpack(lambda r: own[r].astype(jnp.float32), flat, rows, width)
    for c in range(width):
        for image in range(images):
            first = image * high
            value = take(flat, first * width + c, high, width) + time_rows[image : image + 1, :]
            cols[c, first : first + high, :] = value
            start_out[c * rows + first : c * rows + first + high, :] = value
    bias = vec(dw_bias)
    base = lambda c, first, lane: jnp.broadcast_to(bias[:, lane : lane + LANES], (high, LANES))
    stencil(cols, own_places(width), taps, base, writer(part_out, rows), False, images, high, width)


def mix_sides_kernel(
    inner, outer, time_rows, taps, part, gain, shift, mixed_out, flat, cols, *, images, high, width
):
    rows = images * high
    position = lax.axis_index("rows")
    odd = position % 2 == 1
    for side in range(2):
        first_tile, second_tile = (inner, outer) if side == 0 else (outer, inner)
        unpack(
            lambda r: jnp.where(odd, first_tile[r].astype(jnp.float32), second_tile[r].astype(jnp.float32)),
            flat, rows, width,
        )
        edge = position > 0 if side == 0 else position < lax.axis_size("rows") - 1
        for i in range(3):
            c = width - 3 + i if side == 0 else i
            for image in range(images):
                first = image * high
                value = take(flat, first * width + c, high, width) + time_rows[image : image + 1, :]
                cols[side * 3 + i, first : first + high, :] = value * jnp.where(edge, 1.0, 0.0)
    stencil(
        cols, side_places(width), taps, reader(part, rows, high), writer(mixed_out, rows), False, images, high, width
    )
    tokens = rows * width
    mixed_out[tokens : tokens + 1, :] = vec(gain)
    mixed_out[tokens + 1 : tokens + 2, :] = vec(shift)


def forward_kernel(
    own, other, slope, up, up_bias, down, branch_out, branch_send, hidden_grad, normed_out, normed_other_out, inverse_out,
    active, *, images, high, width, full, chunk
):
    tokens = images * high * width
    half = own.shape[1]
    hidden_size = up.shape[1]
    index = lax.axis_index("chan")
    mine = pl.multiple_of(index * half, half)
    theirs = pl.multiple_of((1 - index) * half, half)
    x = own[:tokens, :]
    y = other[:tokens, :]
    mean = (jnp.sum(x, 1, keepdims=True) + jnp.sum(y, 1, keepdims=True)) / full
    square = (jnp.sum(x * x, 1, keepdims=True) + jnp.sum(y * y, 1, keepdims=True)) / full
    inverse = lax.rsqrt(square - mean * mean + EPSILON)
    normed_x = (x - mean) * inverse
    normed_y = (y - mean) * inverse
    scaled_x = normed_x * own[tokens : tokens + 1, :] + own[tokens + 1 : tokens + 2, :]
    scaled_y = normed_y * other[tokens : tokens + 1, :] + other[tokens + 1 : tokens + 2, :]
    scaled_x = scaled_x.astype(jnp.bfloat16)
    scaled_y = scaled_y.astype(jnp.bfloat16)
    normed_out[...] = normed_x
    normed_other_out[...] = normed_y
    inverse_out[...] = jnp.broadcast_to(inverse, inverse_out.shape)
    bias = vec(up_bias)
    for j in range(0, hidden_size, chunk):
        hidden = jnp.dot(scaled_x, up[pl.ds(mine, half), j : j + chunk], preferred_element_type=jnp.float32)
        hidden = hidden + jnp.dot(
            scaled_y, up[pl.ds(theirs, half), j : j + chunk], preferred_element_type=jnp.float32
        )
        hidden = hidden + bias[:, j : j + chunk]
        cell = hidden * hidden
        tangent = jnp.tanh(KAPPA * (hidden + CUBIC * cell * hidden))
        grown = 0.5 * (1.0 + tangent)
        active[:, j : j + chunk] = (hidden * grown).astype(jnp.bfloat16)
        steep = grown + 0.5 * hidden * (1.0 - tangent * tangent) * KAPPA * (1.0 + 3.0 * CUBIC * cell)
        for c in range(width):
            for image in range(images):
                first = (c * images + image) * high
                hidden_grad[first : first + high, j : j + chunk] = (
                    slope[image : image + 1, j : j + chunk] * steep[first : first + high, :]
                ).astype(jnp.bfloat16)
    live = active[...]
    branch_send[...] = jnp.dot(live, down[:, pl.ds(theirs, half)], preferred_element_type=jnp.float32)
    branch_out[...] = jnp.dot(live, down[:, pl.ds(mine, half)], preferred_element_type=jnp.float32)


def backward_kernel(
    hidden_grad, up, own, other, normed, normed_other, grad_out, grad_send, sums_out
):
    tokens, half = normed.shape
    index = lax.axis_index("chan")
    mine = pl.multiple_of(index * half, half)
    theirs = pl.multiple_of((1 - index) * half, half)
    back = hidden_grad[...]
    across = (((1,), (1,)), ((), ()))
    grad_y = lax.dot_general(back, up[pl.ds(theirs, half), :], across, preferred_element_type=jnp.float32)
    grad_x = lax.dot_general(back, up[pl.ds(mine, half), :], across, preferred_element_type=jnp.float32)
    grad_send[:, :half] = grad_y.astype(jnp.bfloat16)
    grad_out[...] = grad_x
    gained_x = grad_x * own[tokens : tokens + 1, :]
    gained_y = grad_y * other[tokens : tokens + 1, :]
    first_sum = jnp.sum(gained_x + gained_y, 1, keepdims=True)
    second_sum = jnp.sum(gained_x * normed[...] + gained_y * normed_other[...], 1, keepdims=True)
    lane = lax.broadcasted_iota(jnp.int32, (tokens, LANES), 1)
    sums = jnp.where(lane % 2 == 0, first_sum, second_sum)
    sums_out[...] = sums
    coarse = sums.astype(jnp.bfloat16).astype(jnp.float32)
    grad_send[:, half:] = jnp.where(lane < 2, coarse, sums - coarse).astype(jnp.bfloat16)


def features_kernel(branch, branch_other, start, down_bias, layer_scale, features_out, flat, *, rows, width):
    tokens, half = branch.shape
    mine = pl.multiple_of(lax.axis_index("chan") * half, half)
    scale = layer_scale[pl.ds(mine, half)].astype(jnp.float32).reshape(1, half)
    features = start[...] + scale * (branch[...] + branch_other[...] + vec(down_bias))
    for c in range(width):
        for l in range(flat.shape[0]):
            flat[l, pl.ds(c, rows, stride=width), :] = features[
                c * rows : (c + 1) * rows, l * LANES : (l + 1) * LANES
            ]
    for r in range(rows):
        features_out[r] = take(flat, r * width, width, 1).astype(jnp.bfloat16)


def norm_grad_kernel(
    grad, grad_other, sums, normed, inverse, gain, grad_out, inner_out, outer_out, *, rows, full
):
    tokens, half = grad.shape
    gained = (grad[...] + grad_other[:, :half].astype(jnp.float32)) * vec(gain)
    extra = grad_other[:, half:].astype(jnp.float32)
    first_sum = (sums[:, 0:1] + (extra[:, 0:1] + extra[:, 2:3])) / full
    second_sum = (sums[:, 1:2] + (extra[:, 1:2] + extra[:, 3:4])) / full
    grad_out[...] = inverse[:, 0:1] * (gained - first_sum - normed[...] * second_sum)
    edge = 3 * rows
    parity = lax.axis_index("rows") % 2
    low = pl.multiple_of(parity * (tokens - edge), 8)
    high = pl.multiple_of((1 - parity) * (tokens - edge), 8)
    inner_out[...] = grad_out[pl.ds(high, edge), :].astype(jnp.bfloat16)
    outer_out[...] = grad_out[pl.ds(low, edge), :].astype(jnp.bfloat16)


def unmix_own_kernel(own, class_rows, taps, part_out, cols, *, images, high, width):
    rows = images * high
    for c in range(width):
        cols[c] = own[c * rows : (c + 1) * rows, :]
    classes = class_rows[...]

    def base(c, first, lane):
        image = first // high
        return jnp.broadcast_to(classes[image : image + 1, lane : lane + LANES], (high, LANES))

    stencil(cols, own_places(width), taps, base, writer(part_out, rows), True, images, high, width)


def unmix_sides_kernel(
    part, inner, outer, taps, features, gradient_out, features_out, flat, cols, lines, *, images, high, width
):
    rows = images * high
    position = lax.axis_index("rows")
    parity = position % 2
    within = (position > 0) & (position < lax.axis_size("rows") - 1)
    for c in range(3):
        cols[(1 - parity) * 3 + c] = inner[c * rows : (c + 1) * rows, :].astype(jnp.float32)
        cols[parity * 3 + c] = outer[c * rows : (c + 1) * rows, :].astype(jnp.float32) * jnp.where(within, 1.0, 0.0)

    def store(c, first, lane, value):
        flat[lane // LANES, pl.ds(first * width + c, high, stride=width), :] = value

    stencil(cols, side_places(width), taps, reader(part, rows, high), store, True, images, high, width)
    for r in range(rows):
        gradient_out[r] = take(flat, r * width, width, 1)
    high_out, wide_out, _ = features_out.shape
    for j in range(high_out):
        for block in range(wide_out // width):
            lines[block * width : (block + 1) * width, :] = features[block * high_out + j].astype(jnp.float32)
        features_out[j] = lines[...].astype(jnp.bfloat16)


def pair_exchange(inner, outer, axis):
    count = lax.axis_size(axis)
    with jax.named_scope("inner"):
        inner = lax.ppermute(inner, axis, [(i, i ^ 1) for i in range(count)])
    with jax.named_scope("outer"):
        outer = lax.ppermute(
            outer, axis, [(i, min(max(((i + 1) ^ 1) - 1, 0), count - 1)) for i in range(count)]
        )
    return inner, outer


def per_device(
    latents,
    timestep,
    label,
    time_table,
    class_table,
    dw_kernel,
    dw_bias,
    ln_gain,
    ln_bias,
    up_weight,
    up_bias,
    down_weight,
    down_bias,
    layer_scale,
):
    rows, width, half = latents.shape
    full = class_table.shape[1]
    images = timestep.shape[0]
    high = rows // images
    tokens = rows * width
    hidden_size = up_weight.shape[1]
    f32 = jnp.float32
    bf16 = jnp.bfloat16
    sizes = dict(images=images, high=high, width=width)
    swap = [(0, 1), (1, 0)]

    with jax.named_scope("latent_halo"):
        inner, outer = pair_exchange(latents, latents, "rows")
    time_rows, class_rows, direction, down = call(
        functools.partial(setup_kernel, images=images, half=half),
        [((8, half), f32), ((8, half), f32), ((8, full), bf16), (down_weight.shape, bf16)],
        [(a, pltpu.HBM) for a in (timestep, label, time_table, class_table, layer_scale, down_weight)],
        [
            pltpu.SMEM(timestep.shape, jnp.int32),
            pltpu.SMEM(label.shape, jnp.int32),
            pltpu.VMEM(class_table.shape, bf16),
            pltpu.VMEM(layer_scale.shape, bf16),
            pltpu.VMEM((images, 8, half), bf16),
            pltpu.SemaphoreType.DMA((5 + images,)),
        ],
        name="setup",
    )
    flat = pltpu.VMEM((half // LANES, tokens, LANES), f32)
    part, start, taps = call(
        functools.partial(mix_own_kernel, **sizes),
        [((tokens, half), f32), ((tokens, half), f32), ((56, half), f32)],
        [latents, time_rows, dw_kernel, dw_bias],
        [flat, pltpu.VMEM((width, rows, half), f32)],
        name="mix_own",
    )
    (mixed,) = call(
        functools.partial(mix_sides_kernel, **sizes),
        [((tokens + 8, half), f32)],
        [inner, outer, time_rows, taps, part, ln_gain, ln_bias],
        [flat, pltpu.VMEM((6, rows, half), f32)],
        name="mix_sides",
    )
    mixed_other = lax.ppermute(mixed, "chan", swap)
    direction, _ = lax.optimization_barrier((direction, mixed))
    (slope,) = call(slope_kernel, [((8, hidden_size), f32)], [direction, down], name="slope")
    branch, branch_send, hidden_grad, normed, normed_other, inverse = call(
        functools.partial(forward_kernel, full=full, chunk=512, **sizes),
        [
            ((tokens, half), f32),
            ((tokens, half), f32),
            ((tokens, hidden_size), bf16),
            ((tokens, half), f32),
            ((tokens, half), f32),
            ((tokens, LANES), f32),
        ],
        [mixed, mixed_other, slope, up_weight, up_bias, down],
        [pltpu.VMEM((tokens, hidden_size), bf16)],
        name="forward",
    )
    branch_other = lax.ppermute(branch_send, "chan", swap)
    grad, grad_send, sums = call(
        backward_kernel,
        [((tokens, half), f32), ((tokens, half + LANES), bf16), ((tokens, LANES), f32)],
        [hidden_grad, up_weight, mixed, mixed_other, normed, normed_other],
        name="backward",
    )
    grad_other = lax.ppermute(grad_send, "chan", swap)
    (features,) = call(
        functools.partial(features_kernel, rows=rows, width=width),
        [((rows, width, half), bf16)],
        [branch, branch_other, start, down_bias, layer_scale],
        [pltpu.VMEM((half // LANES, tokens, LANES), f32)],
        name="join",
    )
    with jax.named_scope("spread"):
        features = lax.all_to_all(features, "rows", split_axis=0, concat_axis=0, tiled=True)
    mixed_grad, inner, outer = call(
        functools.partial(norm_grad_kernel, rows=rows, full=full),
        [((tokens, half), f32), ((3 * rows, half), bf16), ((3 * rows, half), bf16)],
        [grad, grad_other, sums, normed, inverse, ln_gain],
        name="norm_grad",
    )
    with jax.named_scope("grad_halo"):
        inner, outer = pair_exchange(inner, outer, "rows")
    (part,) = call(
        functools.partial(unmix_own_kernel, **sizes),
        [((tokens, half), f32)],
        [mixed_grad, class_rows, taps],
        [pltpu.VMEM((width, rows, half), f32)],
        name="unmix_own",
    )
    count = lax.axis_size("rows")
    gradient, features = call(
        functools.partial(unmix_sides_kernel, **sizes),
        [((rows, width, half), f32), ((rows // count, width * count, half), bf16)],
        [part, inner, outer, taps, features],
        [flat, pltpu.VMEM((6, rows, half), f32), pltpu.VMEM((width * count, half), f32)],
        name="unmix_sides",
    )
    return features, gradient


def solution(mesh):
    in_specs = (
        P("groups", "rows", "chan"),
        P("groups"),
        P("groups"),
        P(None, "chan"),
        P(),
        P(None, None, "chan"),
        P("chan"),
        P("chan"),
        P("chan"),
        P(None, "chan"),
        P("chan"),
        P("chan", None),
        P("chan"),
        P(),
    )
    out_specs = (P(("groups", "rows"), None, "chan"), P("groups", "rows", "chan"))
    return jax.shard_map(
        per_device, mesh=mesh, in_specs=in_specs, out_specs=out_specs, check_vma=False
    )
```
